32 devices in a mesh: replica: 8 (over y, x, core), shard: 4 (over z).
Axes of the slice: x: 2, y: 2, z: 4, core: 2. Of those that a mesh axis runs over, the one named last changes fastest.
Arguments:
- images: bfloat16 [96, 320, 1024], P(('replica', 'shard')), may hold values from -6 to 6
- teacher: bfloat16 [96, 320, 1024], P(('replica', 'shard')), may hold values from -6 to 6
- keep_mask: int32 [96, 320], P(('replica', 'shard')), may hold values from 0 to 1, as said below
- ln1_gain: bfloat16 [1024], P('shard'), may hold values from 0.5 to 1.5
- ln1_bias: bfloat16 [1024], P('shard'), may hold values from -1 to 1
- qkv_weight: bfloat16 [1024, 3072], P('shard'), may hold values from -0.1875 to 0.1875
- qv_bias: bfloat16 [2048], P('shard'), may hold values from -1 to 1
- out_weight: bfloat16 [1024, 1024], P('shard'), may hold values from -0.5 to 0.5
- out_bias: bfloat16 [1024], P('shard'), may hold values from -1.5 to 1.5
- ln2_gain: bfloat16 [1024], P('shard'), may hold values from 0.5 to 1.5
- ln2_bias: bfloat16 [1024], P('shard'), may hold values from -1 to 1
- fc1_weight: bfloat16 [1024, 4096], P('shard'), may hold values from -0.1875 to 0.1875
- fc1_bias: bfloat16 [4096], P('shard'), may hold values from -1.5 to 1.5
- fc2_weight: bfloat16 [4096, 1024], P('shard'), may hold values from -0.09375 to 0.09375
- fc2_bias: bfloat16 [1024], P('shard'), may hold values from -1.5 to 1.5
Outputs:
- layer_out: bfloat16 [96, 320, 1024], P(('replica', 'shard'))
- input_grad: float32 [96, 320, 1024], P(('replica', 'shard'))
- loss: float32 [], replicated
- ln1_gain_grad: float32 [1024], P('shard')
- ln1_bias_grad: float32 [1024], P('shard')
- qkv_weight_grad: float32 [1024, 3072], P('shard')
- qv_bias_grad: float32 [2048], P('shard')
- out_weight_grad: float32 [1024, 1024], P('shard')
- out_bias_grad: float32 [1024], P('shard')
- ln2_gain_grad: float32 [1024], P('shard')
- ln2_bias_grad: float32 [1024], P('shard')
- fc1_weight_grad: float32 [1024, 4096], P('shard')
- fc1_bias_grad: float32 [4096], P('shard')
- fc2_weight_grad: float32 [4096, 1024], P('shard')
- fc2_bias_grad: float32 [1024], P('shard')
The draws below stay inside these ranges and needn't reach their ends.
Inputs may be any that keep to these rules, and one draw needn't show every extreme that they name: `keep_mask`: the first 64 positions of every image are always kept.
All inputs are finite; a program needn't handle non-finite values.
Results may differ from the reference program's by a relative error of at most 0.007.
Values may be sent and summed in bfloat16 or wider, within the bound.
No kernel may reach another device: no remote copies, remote signals or barrier semaphores. Data moves between devices by JAX's collectives and lax.ppermute only.
A program may use at most 256 MiB of HBM per device.

```python
import math
import jax
import jax.numpy as jnp
from jax import lax

D = 1024
H = 16
HD = 64
FF = 4096
PATCHES = 256
BUFFER = 64
SEQ = 320
IMAGES = 96
TOKENS = 30720


def draw_keep_mask(key, part):
    position = jnp.arange(IMAGES, dtype=jnp.int32)
    fewest = PATCHES // 16
    most_kept = PATCHES * 7 // 8
    base_kept = fewest + (most_kept - fewest) * position // max(IMAGES - 1, 1)
    jitter = jax.random.randint(jax.random.fold_in(key, 1), (IMAGES,), 0, PATCHES // 16 + 1)
    kept_count = jnp.minimum(base_kept + jitter, PATCHES)
    image_keys = jax.random.split(jax.random.fold_in(key, 2), IMAGES)
    ranks = jax.vmap(lambda image_key: jax.random.permutation(image_key, PATCHES))(image_keys)
    patch_keep = (ranks < kept_count[:, None]).astype(jnp.int32)
    buffer_keep = jnp.ones((IMAGES, BUFFER), jnp.int32)
    return jnp.concatenate([buffer_keep, patch_keep], axis=1)


def steps_of(stream_key, dims, shards, least, largest):
    def one(dim, blocks):
        heights = jax.random.uniform(jax.random.fold_in(jax.random.fold_in(stream_key, 6), dim), (blocks,), jnp.float32, least / len(shards), largest / len(shards))
        return jnp.repeat(jnp.exp(heights), dims[dim] // blocks).reshape((-1,) + (1,) * (len(dims) - dim - 1))

    gain = one(*shards[0])
    for cut in shards[1:]:
        gain = gain * one(*cut)
    return gain


def noise(key, extent, scale, reach, cuts=(), kind=jnp.bfloat16):
    entries = scale * jax.random.normal(key, extent, jnp.float32)
    if cuts:
        entries = entries * steps_of(key, extent, cuts, -0.22, 0.18)
    return jnp.clip(entries, -reach, reach).astype(kind)


def setup_inputs(seed: int = 0) -> dict:
    arg_keys = jax.random.split(jax.random.key(seed), 16)
    return {
        "images": noise(arg_keys[0], (IMAGES, SEQ, D), 1.0, 6.0, ((0, 32),)),
        "teacher": noise(arg_keys[1], (IMAGES, SEQ, D), 1.0, 6.0, ((0, 32),)),
        "keep_mask": draw_keep_mask(jax.random.fold_in(arg_keys[15], 71), 0),
        "ln1_gain": jnp.clip(1.0 + 0.1 * jax.random.normal(arg_keys[3], (D,), jnp.float32), 0.5, 1.5).astype(jnp.bfloat16),
        "ln1_bias": noise(arg_keys[4], (D,), 0.2, 1.0, ((0, 4),)),
        "qkv_weight": noise(arg_keys[5], (D, 3 * D), D ** -0.5, 0.1875, ((0, 4),)),
        "qv_bias": noise(arg_keys[6], (2 * D,), 0.2, 1.0, ((0, 4),)),
        "out_weight": noise(arg_keys[7], (D, D), (D // 8) ** -0.5, 0.5, ((0, 4),)),
        "out_bias": noise(arg_keys[8], (D,), 0.3, 1.5, ((0, 4),)),
        "ln2_gain": jnp.clip(1.0 + 0.1 * jax.random.normal(arg_keys[9], (D,), jnp.float32), 0.5, 1.5).astype(jnp.bfloat16),
        "ln2_bias": noise(arg_keys[10], (D,), 0.2, 1.0, ((0, 4),)),
        "fc1_weight": noise(arg_keys[11], (D, FF), D ** -0.5, 0.1875, ((0, 4),)),
        "fc1_bias": noise(arg_keys[12], (FF,), 0.3, 1.5, ((0, 4),)),
        "fc2_weight": noise(arg_keys[13], (FF, D), FF ** -0.5, 0.09375, ((0, 4),)),
        "fc2_bias": noise(arg_keys[14], (D,), 0.3, 1.5, ((0, 4),)),
    }


@jax.custom_vjp
def low(v):
    return lax.optimization_barrier(v.astype(jnp.bfloat16)).astype(jnp.float32)

@jax.custom_vjp
def low_back(v):
    return v

def low_keep(v):
    return (low(v), None)

def low_pass(kept, grad):
    return (grad,)

def back_keep(v):
    return (v, None)

def back_low(kept, grad):
    return (low(grad),)
low.defvjp(low_keep, low_pass)
low_back.defvjp(back_keep, back_low)
EPS = 1e-06
NEG = -1e+30
HIGH = lax.Precision.HIGHEST

def layer_norm(row_data, gain_vec, shift_vec):
    average = lax.optimization_barrier(jnp.mean(row_data, axis=-1, keepdims=True))
    centred = row_data - average
    spread = lax.optimization_barrier(jnp.mean(centred * centred, axis=-1, keepdims=True))
    return centred * lax.rsqrt(spread + EPS) * gain_vec + shift_vec

def project(left_side, right_side):
    return jnp.einsum('gsd,de->gse', left_side, right_side, precision=HIGH)

def forward(params, image_rows, teacher_rows, keep_rows):
    ln1_gain, ln1_bias, qkv_weight, qv_bias, out_weight, out_bias, ln2_gain, ln2_bias, fc1_weight, fc1_bias, fc2_weight, fc2_bias = params
    normed_one = low(layer_norm(image_rows, ln1_gain, ln1_bias))
    projected = project(normed_one, qkv_weight)
    query_rows = low(low_back(projected[..., :D] + qv_bias[:D]))
    key_rows = low(low_back(projected[..., D:2 * D]))
    value_rows = low(low_back(projected[..., 2 * D:] + qv_bias[D:]))
    head_shape = image_rows.shape[:2] + (H, HD)
    query_heads = query_rows.reshape(head_shape)
    key_heads = key_rows.reshape(head_shape)
    value_heads = value_rows.reshape(head_shape)
    raw_scores = low_back(jnp.einsum('gqhe,gkhe->ghqk', query_heads, key_heads, precision=HIGH) * (1.0 / math.sqrt(HD)))
    scores = jnp.where(keep_rows[:, None, None, :] > 0, raw_scores, NEG)
    row_top = lax.optimization_barrier(jnp.max(scores, axis=-1, keepdims=True))
    exponent = jnp.exp(scores - row_top)
    probs = exponent / lax.optimization_barrier(jnp.sum(exponent, axis=-1, keepdims=True))
    mixed_heads = jnp.einsum('ghqk,gkhe->gqhe', low(probs), value_heads, precision=HIGH).reshape(image_rows.shape)
    mixed_heads = low(low_back(mixed_heads))
    attn_out = low_back(project(mixed_heads, out_weight) + out_bias)
    residual = image_rows + attn_out
    normed_two = low(layer_norm(residual, ln2_gain, ln2_bias))
    hidden_pre = low_back(project(normed_two, fc1_weight) + fc1_bias)
    hidden_act = low(jax.nn.gelu(hidden_pre, approximate=False))
    branch_out = low_back(project(hidden_act, fc2_weight) + fc2_bias)
    layer_rows = residual + branch_out
    errors = layer_rows - teacher_rows
    squares = jnp.sum(keep_rows[..., None] * errors * errors)
    return (layer_rows, squares)

def reference(images, teacher, keep_mask, ln1_gain, ln1_bias, qkv_weight, qv_bias, out_weight, out_bias, ln2_gain, ln2_bias, fc1_weight, fc1_bias, fc2_weight, fc2_bias):
    params = tuple((item.astype(jnp.float32) for item in (ln1_gain, ln1_bias, qkv_weight, qv_bias, out_weight, out_bias, ln2_gain, ln2_bias, fc1_weight, fc1_bias, fc2_weight, fc2_bias)))
    kept_total = jnp.sum(keep_mask).astype(jnp.float32)
    factor = TOKENS / (2.0 * kept_total)
    blocks = IMAGES // 8
    image_blocks = images.reshape(blocks, 8, SEQ, D)
    teacher_blocks = teacher.reshape(blocks, 8, SEQ, D)
    keep_blocks = keep_mask.reshape(blocks, 8, SEQ)

    def one_group(totals, item):
        image_part, teacher_part, keep_part = item

        def apply(weights, inputs):
            return forward(weights, inputs, teacher_part.astype(jnp.float32), keep_part)
        (layer_rows, squares), pull = jax.vjp(apply, params, image_part.astype(jnp.float32))
        param_grads, inputs_grad = pull((jnp.zeros_like(layer_rows), factor.astype(squares.dtype)))
        totals = jax.tree.map(jnp.add, totals, param_grads)
        return (totals, (layer_rows.astype(jnp.bfloat16), inputs_grad, squares))
    start = tuple((jnp.zeros_like(item) for item in params))
    totals, (layer_parts, grad_parts, square_parts) = lax.scan(one_group, start, (image_blocks, teacher_blocks, keep_blocks))
    loss_value = jnp.sum(square_parts) / (D * kept_total)
    return (layer_parts.reshape(IMAGES, SEQ, D), grad_parts.reshape(IMAGES, SEQ, D), loss_value, totals[0], totals[1], totals[2], totals[3], totals[4], totals[5], totals[6], totals[7], totals[8], totals[9], totals[10], totals[11])
```

```python
import functools

import jax
import jax.numpy as jnp
from jax import lax
from jax.experimental import pallas as pl
from jax.experimental.pallas import tpu as pltpu
from jax.sharding import PartitionSpec as P

H = 16
HD = 64
EPS = 1e-06
NEG = -1e30
LANES = 128
BF = jnp.bfloat16
F32 = jnp.float32


def layer_norm(row_data, gain_vec, shift_vec):
    average = jnp.mean(row_data, axis=-1, keepdims=True)
    centred = row_data - average
    spread = jnp.mean(centred * centred, axis=-1, keepdims=True)
    return centred * lax.rsqrt(spread + EPS) * gain_vec + shift_vec


def gelu_exact(values):
    return jax.nn.gelu(values, approximate=False)


def column_sum(row_data):
    return jnp.sum(row_data.astype(F32), axis=0)


def dot(left_side, right_side):
    return jnp.dot(left_side, right_side, preferred_element_type=F32)


def transposed(left_side, right_side):
    return lax.dot_general(
        left_side, right_side, (((0,), (0,)), ((), ())), preferred_element_type=F32
    )


def against(left_side, right_side):
    return lax.dot_general(
        left_side, right_side, (((1,), (1,)), ((), ())), preferred_element_type=F32
    )


def flip(value, axis, bit):
    size = lax.axis_size(axis)
    return lax.ppermute(value, axis, [(i, i ^ bit) for i in range(size)])


def bits_of(size):
    return [1 << b for b in range(size.bit_length() - 1)]


def shard_stage(own):
    stack = own[None]
    for bit in bits_of(lax.axis_size("shard")):
        stack = jnp.concatenate([stack, flip(stack, "shard", bit)], axis=0)
    return stack


def plane_stage(block, chip_bits):
    stack, offsets = block[None], [0]
    for bit in chip_bits[:-1]:
        stack = jnp.concatenate([stack, flip(stack, "replica", bit)], axis=0)
        offsets = offsets + [j ^ bit for j in offsets]
    parts = [(offsets, stack)]
    last = chip_bits[-1]
    parts.append(([j ^ last for j in offsets], flip(stack, "replica", last)))
    return parts + [([j ^ 1 for j in js], flip(a, "replica", 1)) for js, a in parts]


def assemble_kernel(where_ref, local_ref, *refs, offsets, width, column):
    parts, out_ref = refs[:-1], refs[-1]
    step = pl.program_id(0)

    @pl.when(step == 0)
    def _():
        out_ref[...] = local_ref[...]

    @pl.when(step > 0)
    def _():
        for js, part in zip(offsets, parts):
            for t, j in enumerate(js):
                place = pl.multiple_of((where_ref[0] ^ j) * width, LANES)
                out_ref[:, pl.ds(place, width)] = part[t, 0, :, column : column + width]


def assemble(local, parts, column, width):
    rows, columns = local.shape
    shards = lax.axis_size("shard")
    r, z = lax.axis_index("replica"), lax.axis_index("shard")
    if width % LANES:
        whole = jnp.zeros((shards * rows, columns), local.dtype)
        whole = lax.dynamic_update_slice(whole, local, (z * rows, 0))
        for js, part in parts:
            for t, j in enumerate(js):
                for d in range(1, shards):
                    piece = part[t, d - 1, :, column : column + width]
                    whole = lax.dynamic_update_slice(
                        whole, piece, ((z ^ d) * rows, (r ^ j) * width)
                    )
        return whole
    where = jnp.stack([r, z]).astype(jnp.int32)
    full = parts[0][1].shape[-1]
    return pl.pallas_call(
        functools.partial(
            assemble_kernel, offsets=[js for js, _ in parts], width=width, column=column
        ),
        out_shape=jax.ShapeDtypeStruct((shards * rows, columns), local.dtype),
        grid_spec=pltpu.PrefetchScalarGridSpec(
            num_scalar_prefetch=1,
            grid=(shards,),
            in_specs=[pl.BlockSpec((rows, columns), lambda d, s: (0, 0))]
            + [
                pl.BlockSpec(
                    (len(js), 1, rows, full), lambda d, s: (0, jnp.maximum(d - 1, 0), 0, 0)
                )
                for js, _ in parts
            ],
            out_specs=pl.BlockSpec((rows, columns), lambda d, s: (s[1] ^ d, 0)),
        ),
        name="assemble",
    )(where, local, *[part for _, part in parts])


def own_columns(value):
    width = value.shape[1] // lax.axis_size("replica")
    return lax.dynamic_slice_in_dim(value, lax.axis_index("replica") * width, width, axis=1)


def halving_order(chip_bits):
    order = [0]
    for bit in list(reversed(chip_bits)) + [1]:
        order = order + [j ^ bit for j in order]
    return order


def weight_grad(left_side, right_side, chip_bits):
    r, z = lax.axis_index("replica"), lax.axis_index("shard")
    members, shards = lax.axis_size("replica"), lax.axis_size("shard")
    width = right_side.shape[1] // members
    order = halving_order(chip_bits)
    pick = lambda js: jnp.concatenate(
        [lax.dynamic_slice_in_dim(right_side, (r ^ j) * width, width, axis=1) for j in js], axis=1
    )
    half = members // 2
    leaving = transposed(left_side, pick(order[half:])).astype(BF)
    arrived = flip(leaving, "replica", 1)
    quarter = half // 2
    sends = transposed(left_side, pick(order[quarter:half]))
    keeps = transposed(left_side, pick(order[:quarter]))
    sends = (sends + arrived[:, quarter * width :].astype(F32)).astype(BF)
    keeps = (keeps + arrived[:, : quarter * width].astype(F32)).astype(BF)
    arrived = flip(sends, "replica", chip_bits[0])
    total = keeps.astype(F32) + arrived.astype(F32)
    for bit in chip_bits[1:]:
        quarter = quarter // 2
        low = total.astype(BF)
        arrived = flip(low[:, quarter * width :], "replica", bit)
        total = low[:, : quarter * width].astype(F32) + arrived.astype(F32)
    low = total.astype(BF)
    rows = low.shape[0] // shards
    stack = [lax.dynamic_slice_in_dim(low, (z ^ d) * rows, rows, axis=0) for d in range(shards)]
    stack = jnp.stack(stack)
    for bit in reversed(bits_of(shards)):
        low = stack.astype(BF)
        arrived = flip(low[bit:], "shard", bit)
        stack = low[:bit].astype(F32) + arrived.astype(F32)
    return stack[0]


def spread_kernel(where_ref, scale_ref, *refs, offsets, width):
    parts, out_ref = refs[:-1], refs[-1]
    for js, part in zip(offsets, parts):
        for t, j in enumerate(js):
            place = pl.multiple_of((where_ref[0] ^ j) * width, LANES)
            out_ref[:, pl.ds(place, width)] = part[t].astype(F32) * scale_ref[0]


def spread(total, chip_bits, scale):
    parts = plane_stage(total.astype(BF), chip_bits)
    rows, width = total.shape
    members = lax.axis_size("replica")
    r = lax.axis_index("replica")

    def finish(factor):
        if width % LANES:
            whole = jnp.zeros((rows, members * width), F32)
            for js, part in parts:
                for t, j in enumerate(js):
                    whole = lax.dynamic_update_slice(
                        whole, part[t].astype(F32) * factor, (0, (r ^ j) * width)
                    )
            return whole
        return pl.pallas_call(
            functools.partial(spread_kernel, offsets=[js for js, _ in parts], width=width),
            out_shape=jax.ShapeDtypeStruct((rows, members * width), F32),
            in_specs=[
                pl.BlockSpec(memory_space=pltpu.SMEM),
                pl.BlockSpec(memory_space=pltpu.SMEM),
            ]
            + [pl.BlockSpec(memory_space=pltpu.VMEM) for _ in parts],
            out_specs=pl.BlockSpec(memory_space=pltpu.VMEM),
            name="spread",
        )(r.astype(jnp.int32)[None], factor[None], *[part for _, part in parts])

    return finish(scale)


def head_lanes(which):
    lane = lax.broadcasted_iota(jnp.int32, (1, LANES), 1)
    return (lane < HD) if which == 0 else (lane >= HD)


def attend_kernel(qkv_ref, mask_ref, mixed_ref, *, features):
    pair = pl.program_id(1)
    at = lambda part: pl.ds(pl.multiple_of(part * features + pair * LANES, LANES), LANES)
    query = qkv_ref[:, at(0)] * BF(HD**-0.5)
    key, value = qkv_ref[:, at(1)], qkv_ref[:, at(2)]
    both = []
    for which in range(2):
        mine = head_lanes(which)
        scores = against(jnp.where(mine, query, BF(0)), key) + mask_ref[0]
        exponent = jnp.exp(scores - jnp.max(scores, axis=1, keepdims=True))
        probs = exponent * (1.0 / jnp.sum(exponent, axis=1, keepdims=True))
        both.append(dot(probs.astype(BF), value))
    mixed_ref[:, pl.ds(pl.multiple_of(pair * LANES, LANES), LANES)] = jnp.where(
        head_lanes(0), both[0], both[1]
    ).astype(BF)


def attend(qkv, mask, length):
    rows, triple = qkv.shape
    features = triple // 3
    images_here = rows // length
    return pl.pallas_call(
        functools.partial(attend_kernel, features=features),
        out_shape=jax.ShapeDtypeStruct((rows, features), BF),
        grid=(images_here, features // LANES),
        in_specs=[
            pl.BlockSpec((length, triple), lambda i, p: (i, 0)),
            pl.BlockSpec((1, 1, length), lambda i, p: (i, 0, 0)),
        ],
        out_specs=pl.BlockSpec((length, features), lambda i, p: (i, 0)),
        name="attend",
    )(qkv, mask[:, None, :])


def attend_back_kernel(qkv_ref, grad_ref, mask_ref, out_ref, *, features):
    pair = pl.program_id(1)
    at = lambda part: pl.ds(pl.multiple_of(part * features + pair * LANES, LANES), LANES)
    query = qkv_ref[:, at(0)] * BF(HD**-0.5)
    key, value = qkv_ref[:, at(1)], qkv_ref[:, at(2)]
    grad = grad_ref[:, pl.ds(pl.multiple_of(pair * LANES, LANES), LANES)]
    outs = []
    for which in range(2):
        mine = head_lanes(which)
        scores = against(jnp.where(mine, key, BF(0)), query) + mask_ref[0]
        exponent = jnp.exp(scores - jnp.max(scores, axis=0, keepdims=True))
        probs = exponent * (1.0 / jnp.sum(exponent, axis=0, keepdims=True))
        probs_grad = against(jnp.where(mine, value, BF(0)), grad)
        inner = jnp.sum(probs * probs_grad, axis=0, keepdims=True)
        score_grad = (probs * (probs_grad - inner)).astype(BF)
        value_grad = dot(probs.astype(BF), grad)
        key_grad = dot(score_grad, query)
        query_grad = transposed(score_grad, key) * (HD**-0.5)
        outs.append((query_grad, key_grad, value_grad))
    for part in range(3):
        out_ref[:, at(part)] = jnp.where(head_lanes(0), outs[0][part], outs[1][part]).astype(BF)


def attend_back(qkv, grad, mask, length):
    rows, triple = qkv.shape
    features = triple // 3
    images_here = rows // length
    return pl.pallas_call(
        functools.partial(attend_back_kernel, features=features),
        out_shape=jax.ShapeDtypeStruct((rows, triple), BF),
        grid=(images_here, features // LANES),
        in_specs=[
            pl.BlockSpec((length, triple), lambda i, p: (i, 0)),
            pl.BlockSpec((length, features), lambda i, p: (i, 0)),
            pl.BlockSpec((1, length, 1), lambda i, p: (i, 0, 0)),
        ],
        out_specs=pl.BlockSpec((length, triple), lambda i, p: (i, 0)),
        name="attend_back",
    )(qkv, grad, mask[:, :, None])


def shards(
    images,
    teacher,
    keep_mask,
    ln1_gain,
    ln1_bias,
    qkv_weight,
    qv_bias,
    out_weight,
    out_bias,
    ln2_gain,
    ln2_bias,
    fc1_weight,
    fc1_bias,
    fc2_weight,
    fc2_bias,
):
    members, groups = lax.axis_size("replica"), lax.axis_size("shard")
    z = lax.axis_index("shard")
    chip_bits = bits_of(members)[1:]
    other_bits = chip_bits[::-1]
    images_here, length, features = images.shape
    row_count = images_here * length

    vectors = (
        ln1_gain,
        ln1_bias,
        qv_bias,
        out_bias,
        ln2_gain,
        ln2_bias,
        fc1_bias,
        fc2_bias,
    )
    sizes = [v.shape[0] for v in vectors]
    packed = jnp.concatenate(vectors)
    own_qkv = own_columns(qkv_weight)
    qkv_rows, qkv_width = own_qkv.shape
    extra = -(-packed.shape[0] // qkv_width)
    packed = jnp.pad(packed, (0, extra * qkv_width - packed.shape[0]))
    stack = shard_stage(jnp.concatenate([own_qkv, packed.reshape(extra, qkv_width)], axis=0))
    around = stack[:, qkv_rows:].reshape(groups, extra * qkv_width)
    ordered = jnp.concatenate(
        [lax.dynamic_slice_in_dim(around, z ^ d, 1, axis=0) for d in range(groups)], axis=0
    ).astype(F32)
    whole_vectors, start = [], 0
    for size in sizes:
        whole_vectors.append(ordered[:, start : start + size].reshape(-1))
        start += size
    gain_one, shift_one, bias_qv, bias_out, gain_two, shift_two, bias_fc1, bias_fc2 = whole_vectors
    parts = plane_stage(stack[1:, :qkv_rows], chip_bits)
    w_qkv = assemble(qkv_weight, parts, 0, qkv_width)

    own_out, own_fc1 = own_columns(out_weight), own_columns(fc1_weight)
    stack = shard_stage(jnp.concatenate([own_out, own_fc1], axis=1))
    parts = plane_stage(stack[1:], other_bits)
    w_out = assemble(out_weight, parts, 0, own_out.shape[1])
    w_fc1 = assemble(fc1_weight, parts, own_out.shape[1], own_fc1.shape[1])

    own_fc2 = own_columns(fc2_weight)
    stack = shard_stage(own_fc2)
    parts = plane_stage(stack[1:], chip_bits)
    w_fc2 = assemble(fc2_weight, parts, 0, own_fc2.shape[1])

    mask = jnp.where(keep_mask > 0, 0.0, NEG).astype(F32)
    keep_rows = keep_mask.reshape(row_count, 1).astype(F32)
    count_here = jnp.sum(keep_mask).astype(F32)
    x_rows = images.reshape(row_count, features).astype(F32)
    normed_one = layer_norm(x_rows, gain_one, shift_one).astype(BF)
    bias_qkv = jnp.concatenate([bias_qv[:features], jnp.zeros_like(bias_qv[:features]), bias_qv[features:]])
    qkv = (dot(normed_one, w_qkv) + bias_qkv).astype(BF)
    mixed = attend(qkv, mask, length)
    residual = x_rows + (dot(mixed, w_out) + bias_out)
    normed_two = layer_norm(residual, gain_two, shift_two).astype(BF)
    hidden_pre = dot(normed_two, w_fc1) + bias_fc1
    hidden_act = gelu_exact(hidden_pre).astype(BF)
    out_full = residual + dot(hidden_act, w_fc2) + bias_fc2
    layer_out = out_full.astype(BF).reshape(images_here, length, features)
    errors = out_full - teacher.reshape(row_count, features).astype(F32)
    out_grad = keep_rows * errors
    squares_here = jnp.sum(out_grad * errors)

    out_low = out_grad.astype(BF)
    grad_bias_fc2 = column_sum(out_low)
    sum_fc2 = weight_grad(hidden_act, out_low, chip_bits)
    act_grad = against(out_low, w_fc2)
    _, gelu_pull = jax.vjp(gelu_exact, hidden_pre)
    pre_grad = gelu_pull(act_grad)[0].astype(BF)
    grad_bias_fc1 = column_sum(pre_grad)
    sum_fc1 = weight_grad(normed_two, pre_grad, other_bits)
    norm_two_grad = against(pre_grad, w_fc1)
    _, second_pull = jax.vjp(layer_norm, residual, gain_two, shift_two)
    residual_part, grad_gain_two, grad_shift_two = second_pull(norm_two_grad)
    residual_grad = out_grad + residual_part
    branch_low = residual_grad.astype(BF)
    grad_bias_out = column_sum(branch_low)
    sum_out = weight_grad(mixed, branch_low, chip_bits)
    mixed_grad = against(branch_low, w_out).astype(BF)
    projected_grad = attend_back(qkv, mixed_grad, mask, length)
    sum_qkv = weight_grad(normed_one, projected_grad, other_bits)
    sums = column_sum(projected_grad)
    grad_bias_qv = jnp.concatenate([sums[:features], sums[2 * features :]])
    norm_one_grad = against(projected_grad, w_qkv)
    _, first_pull = jax.vjp(layer_norm, x_rows, gain_one, shift_one)
    input_part, grad_gain_one, grad_shift_one = first_pull(norm_one_grad)
    input_grad = residual_grad + input_part

    vector_grads = (
        grad_gain_one,
        grad_shift_one,
        grad_bias_qv,
        grad_bias_out,
        grad_gain_two,
        grad_shift_two,
        grad_bias_fc1,
        grad_bias_fc2,
    )
    small = jnp.concatenate([g.reshape(groups, -1) for g in vector_grads], axis=1)
    tail = jnp.zeros((groups, LANES), F32).at[0, 0].set(squares_here).at[0, 1].set(count_here)
    small = jnp.concatenate([small, tail], axis=1)
    for bit in bits_of(members):
        small = small + flip(small, "replica", bit)
    for bit in bits_of(groups):
        small = small + flip(small, "shard", bit)
    squares, kept_total = small[0, -LANES], small[0, -LANES + 1]
    scale = (row_count * members * groups) / kept_total
    loss_value = squares / (features * kept_total)
    mine = lax.dynamic_slice_in_dim(small, z, 1, axis=0)[0] * scale
    finals, start = [], 0
    for size in sizes:
        finals.append(mine[start : start + size])
        start += size
    (
        final_gain_one,
        final_shift_one,
        final_bias_qv,
        final_bias_out,
        final_gain_two,
        final_shift_two,
        final_bias_fc1,
        final_bias_fc2,
    ) = finals
    final_fc2 = spread(sum_fc2, chip_bits, scale)
    final_fc1 = spread(sum_fc1, other_bits, scale)
    final_out = spread(sum_out, chip_bits, scale)
    final_qkv = spread(sum_qkv, other_bits, scale)
    return (
        layer_out,
        (input_grad * scale).reshape(images_here, length, features),
        loss_value,
        final_gain_one,
        final_shift_one,
        final_qkv,
        final_bias_qv,
        final_out,
        final_bias_out,
        final_gain_two,
        final_shift_two,
        final_fc1,
        final_bias_fc1,
        final_fc2,
        final_bias_fc2,
    )


def solution(mesh):
    rows = P(("replica", "shard"), None, None)
    vector, matrix = P("shard"), P("shard", None)
    return jax.shard_map(
        shards,
        mesh=mesh,
        in_specs=(
            rows,
            rows,
            P(("replica", "shard"), None),
            vector,
            vector,
            matrix,
            vector,
            matrix,
            vector,
            vector,
            vector,
            matrix,
            vector,
            matrix,
            vector,
        ),
        out_specs=(
            rows,
            rows,
            P(),
            vector,
            vector,
            matrix,
            vector,
            matrix,
            vector,
            vector,
            vector,
            matrix,
            vector,
            matrix,
            vector,
        ),
        check_vma=False,
    )
```
